512 devices in a mesh: image: 16 (over z, core), ri: 32 (over y, x).
Axes of the slice: x: 4, y: 8, z: 8, core: 2. Of those that a mesh axis runs over, the one named last changes fastest.
Arguments:
- blocks: bfloat16 [16384, 64, 256], P(('image', 'ri')), may hold values from -2.5 to 2.5
- block_owner: int32 [16384, 1], P(('image', 'ri')), may hold values from 0 to 31; in each aligned block of 32 rows (0 to 31, 32 to 63, ...) at most 2 rows name the same one
- block_basis: int32 [16384, 2], P(('image', 'ri')), may hold values from 0 to 255
- pair_images: int32 [16384, 2, 4], P(('image', 'ri')), may hold values from 0 to 15
- pair_cell: int32 [16384, 4], P(('image', 'ri')), may hold values from 0 to 3
- lattice: int32 [4, 2], replicated, may hold values from -3 to 3
- dens_occ: bfloat16 [16, 256, 64], P('image'), may hold values from -1.5 to 1.5
- dens_virt: bfloat16 [16, 256, 64], P('image'), may hold values from -1.5 to 1.5
Outputs:
- chi_k: float32 [2, 64, 32, 256, 256], P(None, None, 'ri', 'image')
The draws below stay inside these ranges and needn't reach their ends.
Inputs may be any that keep to these rules, and one draw needn't show every extreme that they name: `block_owner`: within the 32 blocks of one device no owner is named by more than 2 blocks.
All inputs are finite; a program needn't handle non-finite values.
Results may differ from the reference program's by a relative error of at most 0.0041.
Values may be sent and summed in bfloat16 or wider, within the bound.
A program may use at most 128 MiB of HBM per device.

```python
import math
import jax
import jax.numpy as jnp
import numpy as np
from jax import lax

RI_DEV = 256
KK = 64
NBLK = 256
NIMG = 16
NLOC = 32
CAP = 2
NPAIR = 4
NCELL = 4
KGRID = 8
KPT = 64
BLOCKS = 16384
N_RI = 32


def with_ends(values, stream_key, least, top_value):
    index_at = [jax.random.randint(jax.random.fold_in(stream_key, axis), (), 0, length) for axis, length in enumerate(values.shape)]
    main_axis = values.shape.index(max(values.shape))
    next_to = index_at[:main_axis] + [(index_at[main_axis] + 1) % values.shape[main_axis]] + index_at[main_axis + 1:]
    return values.at[tuple(index_at)].set(least).at[tuple(next_to)].set(top_value)


def with_spikes(entries, rng, source, target, parts, factor):
    owner, partner = [(jnp.arange(entries.shape[dim]) // (entries.shape[dim] // parts)).reshape([-1 if axis == dim else 1 for axis in range(entries.ndim)]) for dim in (source, target)]
    chosen = jax.random.permutation(rng, parts)[partner]
    strong = (owner == chosen) | (owner == (partner + parts // 2) % parts)
    return jnp.where(strong, factor * entries, entries)


def levels(rng, dims, cuts, least, high):
    factor_of = 1.0
    for position, parts in cuts:
        draws = jax.random.uniform(jax.random.fold_in(jax.random.fold_in(rng, 6), position), (parts,), jnp.float32, least / len(cuts), high / len(cuts))
        factor_of = factor_of * jnp.repeat(jnp.exp(draws), dims[position] // parts).reshape((-1,) + (1,) * (len(dims) - 1 - position))
    return factor_of


def deal_out(own_key, own, number, rows, count, top, limit, skew):
    sequence = jax.random.permutation(own_key, count)
    packed, ordinary = portions_of(count, rows * top, limit, skew, True), portions_of(count, rows * top, limit, skew, False)
    places = jnp.arange(count)

    def named(tallies, rotation):
        used = int((tallies > 0).sum())
        fixed = max(1, used // 4)
        shifted = fixed + (places - fixed + rotation * (used - fixed)) % max(1, count - fixed)
        return jnp.zeros((count,), jnp.int32).at[sequence[jnp.where(places < fixed, places, shifted)]].set(jnp.asarray(tallies, jnp.int32))

    tallies = jnp.where(number % 4 == 0, named(packed, number // 4), named(ordinary, number - number // 4 - 1))
    mixed = jax.random.permutation(jax.random.fold_in(own, 3), count)
    donor, taker = mixed[0:count // 2 * 2:2], mixed[1:count // 2 * 2:2]
    slack = jnp.minimum(tallies[donor] - 1, limit - tallies[taker]) // 2
    slack = jnp.where((donor == sequence[0]) | (taker == sequence[0]) | (tallies[taker] == 0), 0, jnp.maximum(slack, 0))
    shifted = jax.random.randint(jax.random.fold_in(own, 4), (count // 2,), 0, 1 << 20) % (slack + 1)
    tallies = tallies.at[donor].add(-shifted).at[taker].add(shifted)
    members = jnp.searchsorted(jnp.cumsum(tallies), jnp.arange(rows * top), side="right").astype(jnp.int32)
    table = members.reshape(top, rows).T
    table = table[jax.random.permutation(jax.random.fold_in(own, 1), rows)]
    rotation = jax.random.randint(jax.random.fold_in(own, 2), (rows, 1), 0, top)
    return jnp.take_along_axis(table, (jnp.arange(top)[None, :] + rotation) % top, axis=1)


def portions_of(amount, total, reach, lean, full):
    weights = [(1 << 20) // math.isqrt(grade ** lean) + 1 for grade in range(1, amount + 1)]
    largest = reach if full else min(reach, max(-(-total // amount), total * weights[0] // sum(weights)))
    least = 1 if total - largest >= amount - 1 else 0
    given, rest = [largest] + [least] * (amount - 1), total - largest - least * (amount - 1)
    while rest > 0:
        candidates = [i for i in range(1, amount) if given[i] < largest] or [i for i in range(1, amount) if given[i] < reach]
        pool, remaining = sum([weights[i] for i in candidates]), rest
        for i in candidates:
            extra = min(reach - given[i], max(1, remaining * weights[i] // pool), rest)
            given[i] = given[i] + extra
            rest = rest - extra
    return np.array(given)


def normal_values(stream_key, shape, scale, bound, cuts=(), held_as=jnp.bfloat16):
    values = jax.random.normal(stream_key, shape, jnp.float32) * scale
    if len(cuts) > 0:
        values = levels(stream_key, shape, cuts, -0.22, 0.18) * values
    return jnp.clip(values, min=-bound, max=bound).astype(held_as)


def gaussian_with(key, shape, spread, reach, cuts, heavy, held_as=jnp.bfloat16):
    drawn = spread * jax.random.normal(key, shape, jnp.float32)
    if cuts:
        drawn = drawn * levels(key, shape, cuts, -0.22, 0.18)
    return jnp.clip(with_spikes(drawn, jax.random.fold_in(key, 3), *heavy), -reach, reach).astype(held_as)


def setup_inputs(seed: int = 0) -> dict:
    key_list = jax.random.split(jax.random.key(seed), 9)
    blocks = gaussian_with(key_list[0], (BLOCKS, KK, RI_DEV), 0.1, 2.5, ((0, 512),), (0, 2, 256, 6.0))
    block_owner_keys = jax.random.split(jax.random.fold_in(key_list[1], 1), BLOCKS // NLOC)
    block_owner_turns = jax.random.permutation(jax.random.fold_in(key_list[1], 3), BLOCKS // NLOC)
    block_owner = jax.vmap(lambda own, number: deal_out(jax.random.fold_in(key_list[1], 2), own, number, NLOC, N_RI, 1, CAP, 2))(block_owner_keys, block_owner_turns).reshape((BLOCKS, 1))
    block_basis = with_ends(jax.random.randint(key_list[2], (BLOCKS, 2), 0, NBLK), jax.random.fold_in(key_list[2], 1), 0, NBLK - 1).astype(jnp.int32)
    pair_images = with_ends(jax.random.randint(key_list[3], (BLOCKS, 2, NPAIR), 0, NIMG), jax.random.fold_in(key_list[3], 1), 0, NIMG - 1).astype(jnp.int32)
    pair_cell = with_ends(jax.random.randint(key_list[4], (BLOCKS, NPAIR), 0, NCELL), jax.random.fold_in(key_list[4], 1), 0, NCELL - 1).astype(jnp.int32)
    lattice = with_ends(jax.random.randint(key_list[5], (NCELL, 2), -3, 4), jax.random.fold_in(key_list[5], 1), -3, 3).astype(jnp.int32)
    dens_occ = normal_values(key_list[6], (NIMG, NBLK, KK), 0.25, 1.5, ((0, 16),))
    dens_virt = normal_values(key_list[7], (NIMG, NBLK, KK), 0.25, 1.5, ((0, 16),))
    return dict(blocks=blocks, block_owner=block_owner, block_basis=block_basis, pair_images=pair_images, pair_cell=pair_cell, lattice=lattice, dens_occ=dens_occ, dens_virt=dens_virt)


def density_terms(running, occ_piece, first_image, virt_whole, listing, pair_count, cell_count):
    image_count, block_count, square = occ_piece.shape
    side_len = math.isqrt(square)
    row_count = listing.shape[0]
    first_block = listing[:, 0]
    second = listing[:, 1]
    occ_img = listing[:, 2:2 + pair_count]
    virt_img = listing[:, 2 + pair_count:2 + 2 * pair_count]
    cell_ids = listing[:, 2 + 2 * pair_count:2 + 3 * pair_count]
    offset = occ_img - first_image
    inside = ((offset >= 0) & (offset < image_count)).astype(jnp.float32)
    occ_rows = (jnp.clip(offset, 0, image_count - 1) * block_count + first_block[:, None]).astype(jnp.int32)
    virt_rows = (virt_img * block_count + second[:, None]).astype(jnp.int32)
    occ_vals = occ_piece.reshape(image_count * block_count, square)[occ_rows].astype(jnp.float32) * inside[:, :, None]
    virt_vals = virt_whole.reshape(-1, square)[virt_rows].astype(jnp.float32)
    select = (cell_ids[:, :, None] == jnp.arange(cell_count, dtype=jnp.int32)[None, None, :]).astype(jnp.float32)
    term_sum = jnp.einsum('sjr,sjlm,sjnq->srlqmn', select, occ_vals.reshape(row_count, pair_count, side_len, side_len), virt_vals.reshape(row_count, pair_count, side_len, side_len), precision=lax.Precision.HIGHEST)
    return running + term_sum.reshape(row_count, cell_count, square, square)

def reference(blocks, block_owner, block_basis, pair_images, pair_cell, lattice, dens_occ, dens_virt):
    listing = jnp.concatenate([block_basis, pair_images[:, 0, :], pair_images[:, 1, :], pair_cell], axis=1).astype(jnp.int32)
    batch_count = BLOCKS // NLOC

    def per_batch(chi_all, pieces):
        blk_part, list_part, own_part = pieces
        zero_ops = jnp.zeros((NLOC, NCELL, KK, KK), jnp.float32)
        density_ops = density_terms(zero_ops, dens_occ, 0, dens_virt, list_part, NPAIR, NCELL).astype(jnp.bfloat16)
        mixed_rows = jnp.einsum('srkm,smp->srkp', density_ops.astype(jnp.float32), blk_part.astype(jnp.float32), precision=lax.Precision.HIGHEST).astype(jnp.bfloat16)
        contrib = jnp.einsum('srkp,skq->srpq', mixed_rows.astype(jnp.float32), blk_part.astype(jnp.float32), precision=lax.Precision.HIGHEST)
        return (chi_all.at[own_part].add(contrib), None)
    chi_start = jnp.zeros((N_RI, NCELL, RI_DEV, RI_DEV), jnp.float32)
    chi_cells, _ = lax.scan(per_batch, chi_start, (blocks.reshape(batch_count, NLOC, KK, RI_DEV), listing.reshape(batch_count, NLOC, -1), block_owner[:, 0].astype(jnp.int32).reshape(batch_count, NLOC)))
    points = jnp.arange(KPT, dtype=jnp.int32)
    wrapped = ((points // KGRID)[:, None] * lattice[None, :, 0] + (points % KGRID)[:, None] * lattice[None, :, 1]) % KGRID
    angles = 2.0 * math.pi / KGRID * wrapped.astype(jnp.float32)
    phases = jnp.concatenate([jnp.cos(angles), jnp.sin(angles)], axis=0)
    result = jnp.einsum('cr,orpq->copq', phases, chi_cells, precision=lax.Precision.HIGHEST)
    return result.reshape(2, KPT, N_RI, RI_DEV, RI_DEV)
```

```python
import functools
import math

import jax
import jax.numpy as jnp
import numpy as np
from jax import lax
from jax.experimental import pallas as pl
from jax.experimental.pallas import tpu as pltpu
from jax.sharding import PartitionSpec as P

KGRID = 8
MESH = pl.DeviceIdType.MESH
NX, NY, NZ, NC = 4, 8, 8, 2
F32, BF16, I32 = jnp.float32, jnp.bfloat16, jnp.int32

ALT = [
    (0, 0), (1, 0), (-1, 0), (0, 1), (0, 3), (1, 1),
    (-1, 3), (1, 3), (-1, 1), (0, 2), (1, 2), (-1, 2),
]
HOME = [
    (0, 0), (2, 2), (-2, 2), (2, 3), (-2, 1), (2, 1), (-2, 3), (1, 2), (-1, 2), (2, 0),
    (-2, 0), (1, 1), (-1, 3), (1, 3), (-1, 1), (0, 2), (0, 1), (0, 3), (1, 0), (-1, 0),
]
NA, NH = len(ALT), len(HOME)
NPAIR = NA + NH


def position():
    i, r = lax.axis_index("image"), lax.axis_index("ri")
    return lax.div(i, NC), lax.rem(i, NC), lax.div(r, NX), lax.rem(r, NX)


def row_of(y, x, dy, dx):
    return lax.rem(y + dy + NY, NY) * NX + lax.rem(x + dx + NX, NX)


def main_kernel(
    lst_ref, occ_ref, virt_ref, blocks_ref, out_ref,
    packa, packh, recva, recvh, lsend, lrecv, pay, idxv, idxs,
    dens, sel, cel, ops, chia, chih,
    sa, sra, sh, srh, za, zra, zh, zrh, ex, exr, lists,
    idx_sem, as_sem, ar_sem, hs_sem, hr_sem, ls_sem, lr_sem,
    ds_sem, dr_sem, fs_sem, fr_sem,
    s_ssem, s_rsem, z_ssem, z_rsem, e_ssem, e_rsem,
):
    z, c, y, x = position()
    image, ri = lax.axis_index("image"), lax.axis_index("ri")
    sib = {"image": z * NC + (1 - c), "ri": ri}
    far = {"image": image, "ri": row_of(y, x, 4, 0)}

    def plane(off, sign=1):
        return {"image": image, "ri": row_of(y, x, sign * off[0], sign * off[1])}

    def zpeer(d):
        return {"image": lax.rem(z + d, NZ) * NC + c, "ri": ri}

    bar = pltpu.get_barrier_semaphore()
    peers = [plane(o) for o in HOME[1:]] + [zpeer(d) for d in range(1, NZ)] + [sib, far]
    for p in peers:
        pl.semaphore_signal(bar, inc=1, device_id=p, device_id_type=MESH)

    dens[image] = jnp.concatenate([occ_ref[0], virt_ref[0]], axis=1)
    lanes = lax.broadcasted_iota(I32, (32, 128), 1)
    erow = lax.broadcasted_iota(I32, (32, 128), 0)
    own = jnp.broadcast_to(lst_ref[:, 14:15], (32, 128)) == lanes
    lo = jnp.min(jnp.where(own, erow, 99), axis=0, keepdims=True)
    hi = jnp.max(jnp.where(own, erow, -1), axis=0, keepdims=True)
    idxv[0:1, :] = jnp.minimum(lo, 31)
    idxv[1:2, :] = jnp.maximum(hi, 0)
    to_smem = pltpu.make_async_copy(idxv, idxs, idx_sem)
    to_smem.start()
    fields = lst_ref[...].astype(F32).astype(BF16)
    for r, hit in ((0, erow == lo), (1, (erow == hi) & (hi != lo))):
        got = lax.dot_general(
            jnp.where(hit, 1.0, 0.0).astype(BF16), fields, (((0,), (0,)), ((), ())),
            preferred_element_type=F32,
        )
        pay[r] = got[0:32].astype(I32)
    for k, o in enumerate(HOME):
        o1, o2 = row_of(y, x, o[0], o[1]), row_of(y, x, o[0] + 4, o[1])
        dst = lrecv if k == 0 else lsend
        for s, (r, q) in enumerate(((0, o1), (1, o1), (0, o2), (1, o2))):
            dst[k, s : s + 1, :] = pay[r, pl.ds(q, 1), :]
    to_smem.wait()

    def pack(offs, shift, buf, local):
        for k, o in enumerate(offs):
            q = row_of(y, x, o[0] + shift, o[1])
            dst = local if k == 0 else buf
            for r in range(2):
                dst[k, r * 64 : (r + 1) * 64, :] = blocks_ref[idxs[r, q]]

    pack(ALT, 4, packa, recva)
    pl.semaphore_wait(bar, len(peers))

    def dcopy(d):
        return pltpu.make_async_remote_copy(
            dens.at[image], dens.at[image], ds_sem.at[d], dr_sem.at[d],
            device_id=zpeer(d), device_id_type=MESH,
        )

    def fcopy(d):
        src = dens.at[lax.rem(z + NZ - d, NZ) * NC + c]
        return pltpu.make_async_remote_copy(
            src, src, fs_sem.at[d], fr_sem.at[d], device_id=sib, device_id_type=MESH
        )

    def lcopy(k):
        return pltpu.make_async_remote_copy(
            lsend.at[k], lrecv.at[k], ls_sem.at[k], lr_sem.at[k],
            device_id=plane(HOME[k]), device_id_type=MESH,
        )

    def acopy(k):
        return pltpu.make_async_remote_copy(
            packa.at[k], recva.at[k], as_sem.at[k], ar_sem.at[k],
            device_id=plane(ALT[k]), device_id_type=MESH,
        )

    def hcopy(k):
        return pltpu.make_async_remote_copy(
            packh.at[k], recvh.at[k], hs_sem.at[k], hr_sem.at[k],
            device_id=plane(HOME[k]), device_id_type=MESH,
        )

    for d in (4, 3, 5, 2, 6, 1, 7):
        dcopy(d).start()
    fcopy(0).start()
    for k in range(1, NH):
        lcopy(k).start()
    for k in range(1, NA):
        acopy(k).start()
    pack(HOME, 0, packh, recvh)
    for k in range(1, NH):
        hcopy(k).start()

    rows2 = lax.broadcasted_iota(I32, (64, 256), 0)
    t = lax.rem(lax.broadcasted_iota(I32, (64, 256), 1), 128)
    xmask = ((t < 64) & (lax.rem(t, 8) == lax.div(rows2, 8))) | (
        (t >= 64) & (lax.div(t - 64, 8) == lax.rem(rows2, 8))
    )
    pi = lax.broadcasted_iota(I32, (256, 256), 0)
    pj = lax.broadcasted_iota(I32, (256, 256), 1)
    pt, u = lax.rem(pi, 128), lax.rem(pj, 64)
    same_r = lax.div(pi, 128) == lax.rem(lax.div(pj, 64), 2)
    occ_part = same_r & (pt < 64) & (pj < 128) & (lax.div(pt, 8) == lax.div(u, 8))
    virt_part = same_r & (pt >= 64) & (pj >= 128) & (lax.rem(pt, 8) == lax.rem(u, 8))
    spread = jnp.where(occ_part | virt_part, 1.0, 0.0).astype(BF16)
    eye = jnp.where(pi == pj, 1.0, 0.0).astype(BF16)

    for k in range(1, NH):
        lcopy(k).wait_recv()
    for n in range(NPAIR):
        k, s = (HOME.index(ALT[n]), 2) if n < NA else (n - NA, 0)
        for r in range(2):
            lists[r * 32 + n : r * 32 + n + 1, :] = lrecv[k, s + r : s + r + 1, :]
    fr = lists[...]
    low = lax.broadcasted_iota(I32, (32, 128), 1) < 64
    for j in range(4):
        cell = jnp.broadcast_to(fr[:, 10 + j : 11 + j], (64, 128))
        cel[j] = jnp.where(low, cell[0:32], cell[32:64])
    basis = lax.broadcasted_iota(I32, (64, 256), 1)
    pick = jnp.concatenate(
        [
            jnp.where(jnp.broadcast_to(fr[:, f : f + 1], (64, 256)) == basis, 1.0, 0.0)
            for f in range(2)
        ],
        axis=0,
    ).astype(BF16)

    for d in (1, 7, 2, 6, 3, 5, 4):
        dcopy(d).wait_recv()
        fcopy(d).start()
    for d in range(NZ):
        fcopy(d).wait_recv()
    sel[...] = jnp.zeros_like(sel)

    def choose(img, carry):
        d = jnp.dot(pick, dens[img], preferred_element_type=F32)
        for j in range(4):
            o_hit = jnp.broadcast_to(lists[:, 2 + j : 3 + j], (64, 128)) == img
            v_hit = jnp.broadcast_to(lists[:, 6 + j : 7 + j], (64, 128)) == img
            lane = lax.broadcasted_iota(I32, (64, 128), 1) < 64
            hit = (o_hit & lane) | (v_hit & jnp.logical_not(lane))
            val = jnp.where(lane, d[0:64], d[64:128])
            for r in range(2):
                rs = slice(r * 32, (r + 1) * 32)
                sel[j, :, r * 128 : (r + 1) * 128] = jnp.where(
                    hit[rs], val[rs], sel[j, :, r * 128 : (r + 1) * 128]
                )
        return carry

    lax.fori_loop(0, NZ * NC, choose, 0)

    def build(n, carry):
        acc = [jnp.zeros((64, 128), F32) for _ in range(4)]
        for j in range(4):
            row = jnp.broadcast_to(sel[j, pl.ds(n, 1), :], (64, 256))
            e = jnp.dot(jnp.where(xmask, row, 0.0).astype(BF16), spread, preferred_element_type=F32)
            kron = e[:, :128] * e[:, 128:]
            cell = jnp.broadcast_to(cel[j, pl.ds(n, 1), :], (64, 128))
            for q in range(4):
                acc[q] = acc[q] + jnp.where(cell == q + 1, kron, 0.0)
        lane = lax.broadcasted_iota(I32, (64, 128), 1) < 64
        for q in range(4):
            ls = slice(q * 128, (q + 1) * 128)
            ops[n, 0:64, ls] = jnp.where(lane, acc[q], 0.0).astype(BF16)
            ops[n, 64:128, ls] = jnp.where(lane, 0.0, acc[q]).astype(BF16)
        return carry

    lax.fori_loop(0, NPAIR, build, 0)

    def group(recv, chi, first, g):
        b = jnp.concatenate([recv[2 * g], recv[2 * g + 1]], axis=0)
        bt = lax.dot_general(eye, b, (((1,), (1,)), ((), ())), preferred_element_type=F32)
        bt = bt.astype(BF16)
        mixed = [
            jnp.dot(
                bt[:, i * 128 : (i + 1) * 128], ops[first + 2 * g + i], preferred_element_type=F32
            ).astype(BF16)
            for i in range(2)
        ]
        for q in range(4):
            ls = slice(q * 128, (q + 1) * 128)
            m = jnp.concatenate([mixed[0][:, ls], mixed[1][:, ls]], axis=1)
            chi[q] += jnp.dot(m, b, preferred_element_type=F32)

    def wait_pair(recv, sem, n):
        pltpu.make_async_remote_copy(
            recv.at[n], recv.at[n], sem.at[n], sem.at[n], device_id=sib, device_id_type=MESH
        ).wait_recv()

    def run_groups(recv, sem, chi, first, start, stop):
        def body(g, carry):
            @pl.when(g > 0)
            def _():
                wait_pair(recv, sem, 2 * g)

            wait_pair(recv, sem, 2 * g + 1)
            group(recv, chi, first, g)
            return carry

        lax.fori_loop(start, stop, body, 0)

    def scopy(buf, rbuf, w):
        return pltpu.make_async_remote_copy(
            buf, rbuf, s_ssem.at[w], s_rsem.at[w], device_id=sib, device_id_type=MESH
        )

    def zcopy(buf, rbuf, w, d):
        return pltpu.make_async_remote_copy(
            buf.at[d], rbuf.at[d], z_ssem.at[w, d], z_rsem.at[w, d],
            device_id=zpeer(d), device_id_type=MESH,
        )

    def share_rows(d, core):
        zz = lax.rem(z + d, NZ)
        return pl.ds(pl.multiple_of((zz * NC + core) * 16, 16), 16)

    def to_sibling(chi, buf, rbuf, w):
        def body(d, carry):
            buf[d] = chi[:, share_rows(d, 1 - c), :].astype(BF16)
            return carry

        lax.fori_loop(0, NZ, body, 0)
        scopy(buf, rbuf, w).start()

    def to_chips(chi, buf, rbuf, zbuf, w):
        scopy(buf, rbuf, w).wait_recv()

        def body(d, carry):
            zbuf[d] = (chi[:, share_rows(d, c), :] + rbuf[d].astype(F32)).astype(BF16)
            return carry

        lax.fori_loop(1, NZ, body, 0)
        return chi[:, share_rows(0, c), :] + rbuf[0].astype(F32)

    chia[...] = jnp.zeros_like(chia)
    chih[...] = jnp.zeros_like(chih)
    run_groups(recva, ar_sem, chia, 0, 0, NA // 2)
    to_sibling(chia, sa, sra, 0)
    run_groups(recvh, hr_sem, chih, NA, 0, 3)
    out_ref[...] = to_chips(chia, sa, sra, za, 0)
    for d in (4, 3, 5, 2, 6, 1, 7):
        zcopy(za, zra, 0, d).start()
    run_groups(recvh, hr_sem, chih, NA, 3, 7)
    total = out_ref[...]
    for d in range(1, NZ):
        zcopy(za, zra, 0, d).wait_recv()
        total = total + zra[d].astype(F32)
    ex[...] = total.astype(BF16)
    to_far = pltpu.make_async_remote_copy(
        ex, exr, e_ssem, e_rsem, device_id=far, device_id_type=MESH
    )
    to_far.start()
    run_groups(recvh, hr_sem, chih, NA, 7, NH // 2)
    to_sibling(chih, sh, srh, 1)
    mine = to_chips(chih, sh, srh, zh, 1)
    for d in (4, 3, 5, 2, 6, 1, 7):
        zcopy(zh, zrh, 1, d).start()
    to_far.wait_recv()
    mine = mine + exr[...].astype(F32)
    for d in (1, 7, 2, 6, 3, 5, 4):
        zcopy(zh, zrh, 1, d).wait_recv()
        mine = mine + zrh[d].astype(F32)
    out_ref[...] = mine

    for d in range(1, NZ):
        dcopy(d).wait_send()
        zcopy(za, zra, 0, d).wait_send()
        zcopy(zh, zrh, 1, d).wait_send()
    for d in range(NZ):
        fcopy(d).wait_send()
    for k in range(1, NH):
        lcopy(k).wait_send()
        hcopy(k).wait_send()
    for k in range(1, NA):
        acopy(k).wait_send()
    scopy(sa, sra, 0).wait_send()
    scopy(sh, srh, 1).wait_send()
    to_far.wait_send()


def phase_kernel(lat_ref, cos_ref, chi_ref, out_ref):
    part = pl.program_id(0)
    n = out_ref.shape[1]

    def body(i, carry):
        k = part * n + i
        k1, k2 = lax.div(k, KGRID), lax.rem(k, KGRID)
        re = jnp.zeros(chi_ref.shape[1:], F32)
        im = jnp.zeros(chi_ref.shape[1:], F32)
        for r in range(chi_ref.shape[0]):
            w = lax.rem(k1 * lat_ref[r, 0] + k2 * lat_ref[r, 1] + 64 * KGRID, KGRID)
            piece = chi_ref[r]
            re = re + cos_ref[w] * piece
            im = im + cos_ref[lax.rem(w + 6, KGRID)] * piece
        out_ref[0, i, 0] = re
        out_ref[1, i, 0] = im
        return carry

    lax.fori_loop(0, n, body, 0, unroll=True)


def local(blocks, block_owner, block_basis, pair_images, pair_cell, lattice, dens_occ, dens_virt):
    rows, square, width = blocks.shape
    cells = lattice.shape[0]
    listing = jnp.concatenate(
        [block_basis, pair_images.reshape(rows, -1), pair_cell + 1, block_owner], axis=1
    )
    listing = jnp.pad(listing, ((0, 0), (0, 128 - listing.shape[1])))
    vm = pltpu.VMEM
    dma = pltpu.SemaphoreType.DMA
    share = (NZ, cells, 16, width)
    chi = pl.pallas_call(
        main_kernel,
        out_shape=jax.ShapeDtypeStruct((cells, 16, width), F32),
        in_specs=[pl.BlockSpec(memory_space=pltpu.VMEM)] * 4,
        out_specs=pl.BlockSpec(memory_space=pltpu.VMEM),
        scratch_shapes=[
            vm((NA, 128, width), BF16),
            vm((NH, 128, width), BF16),
            vm((NA, 128, width), BF16),
            vm((NH, 128, width), BF16),
            vm((NH, 8, 128), I32),
            vm((NH, 8, 128), I32),
            vm((2, 32, 128), I32),
            vm((8, 128), I32),
            pltpu.SMEM((8, 128), I32),
            vm((NZ * NC, 256, 128), BF16),
            vm((4, NPAIR, 256), F32),
            vm((4, NPAIR, 128), I32),
            vm((NPAIR, 128, 512), BF16),
            vm((cells, width, width), F32),
            vm((cells, width, width), F32),
        ]
        + [vm(share, BF16)] * 8
        + [vm(share[1:], BF16)] * 2
        + [vm((64, 128), I32)]
        + [
            dma(()),
            dma((NA,)), dma((NA,)), dma((NH,)), dma((NH,)), dma((NH,)), dma((NH,)),
            dma((NZ,)), dma((NZ,)), dma((NZ,)), dma((NZ,)),
            dma((2,)), dma((2,)), dma((2, NZ)), dma((2, NZ)), dma(()), dma(()),
        ],
        compiler_params=pltpu.CompilerParams(
            collective_id=0, has_side_effects=True, vmem_limit_bytes=48 << 20
        ),
    )(listing, dens_occ, dens_virt, blocks)
    table = jnp.asarray(np.cos(2.0 * math.pi / KGRID * np.arange(KGRID)), F32)
    points = KGRID * KGRID
    parts = 8
    return pl.pallas_call(
        phase_kernel,
        out_shape=jax.ShapeDtypeStruct((2, points, 1, 16, width), F32),
        grid=(parts,),
        in_specs=[
            pl.BlockSpec(memory_space=pltpu.SMEM),
            pl.BlockSpec(memory_space=pltpu.SMEM),
            pl.BlockSpec((cells, 16, width), lambda i: (0, 0, 0)),
        ],
        out_specs=pl.BlockSpec((2, points // parts, 1, 16, width), lambda i: (0, i, 0, 0, 0)),
    )(lattice, table, chi)


def solution(mesh):
    both = ("image", "ri")
    placed = (
        P(both, None, None),
        P(both, None),
        P(both, None),
        P(both, None, None),
        P(both, None),
        P(),
        P("image", None, None),
        P("image", None, None),
    )
    return jax.shard_map(
        local,
        mesh=mesh,
        in_specs=placed,
        out_specs=P(None, None, "ri", "image", None),
        check_vma=False,
    )
```

```python
import functools
import math

import jax
import jax.numpy as jnp
import numpy as np
from jax import lax
from jax.experimental import pallas as pl
from jax.experimental.pallas import tpu as pltpu
from jax.sharding import PartitionSpec as P

KGRID = 8
MESH = pl.DeviceIdType.MESH
NX, NY, NZ, NC = 4, 8, 8, 2
F32, BF16, I32 = jnp.float32, jnp.bfloat16, jnp.int32

ALT = [
    (0, 0), (1, 0), (-1, 0), (0, 1), (0, 3), (1, 1),
    (-1, 3), (1, 3), (-1, 1), (0, 2), (1, 2), (-1, 2),
]
HOME = [
    (0, 0), (2, 2), (-2, 2), (2, 3), (-2, 1), (2, 1), (-2, 3), (1, 2), (-1, 2), (2, 0),
    (-2, 0), (1, 1), (-1, 3), (1, 3), (-1, 1), (0, 2), (0, 1), (0, 3), (1, 0), (-1, 0),
]
NA, NH = len(ALT), len(HOME)
NPAIR = NA + NH


def position():
    i, r = lax.axis_index("image"), lax.axis_index("ri")
    return lax.div(i, NC), lax.rem(i, NC), lax.div(r, NX), lax.rem(r, NX)


def row_of(y, x, dy, dx):
    return lax.rem(y + dy + NY, NY) * NX + lax.rem(x + dx + NX, NX)


def main_kernel(
    owner_hbm, basis_hbm, images_hbm, cell_hbm, occ_hbm, virt_hbm, blocks_hbm, out_hbm,
    owner_ref, basis_ref, images_ref, cell_ref, blk, out_ref,    packa, packh, recva, recvh, lsend, lrecv, pay, idxv, idxs,
    dens, sel, want, cel, ops, chia, chih,
    sa, sra, sh, srh, za, zra, zh, zrh, ex, exr, lists,
    in_sem, idx_sem, as_sem, ar_sem, hs_sem, hr_sem, ls_sem, lr_sem,
    ds_sem, dr_sem, fs_sem, fr_sem,
    s_ssem, s_rsem, z_ssem, z_rsem, e_ssem, e_rsem,
):
    z, c, y, x = position()
    image, ri = lax.axis_index("image"), lax.axis_index("ri")
    sib = {"image": z * NC + (1 - c), "ri": ri}
    far = {"image": image, "ri": row_of(y, x, 4, 0)}

    def plane(off, sign=1):
        return {"image": image, "ri": row_of(y, x, sign * off[0], sign * off[1])}

    def zpeer(d):
        return {"image": lax.rem(z + d, NZ) * NC + c, "ri": ri}

    loads = [
        pltpu.make_async_copy(src, dst, in_sem.at[i])
        for i, (src, dst) in enumerate(
            (
                (owner_hbm, owner_ref),
                (basis_hbm, basis_ref),
                (images_hbm, images_ref),
                (cell_hbm, cell_ref),
                (occ_hbm.at[0], dens.at[image, 0:64]),
                (virt_hbm.at[0], dens.at[image, 64:128]),
                (blocks_hbm, blk),
            )
        )
    ]
    for cp in loads:
        cp.start()

    bar = pltpu.get_barrier_semaphore()
    peers = [plane(o) for o in HOME[1:]] + [zpeer(d) for d in range(1, NZ)] + [sib, far]
    for p in peers:
        pl.semaphore_signal(bar, inc=1, device_id=p, device_id_type=MESH)

    for cp in loads[:4]:
        cp.wait()
    orow = lax.broadcasted_iota(I32, (32, 32), 0)
    ecol = lax.broadcasted_iota(I32, (32, 32), 1)
    own = jnp.broadcast_to(owner_ref[...], (32, 32)) == orow
    lo = jnp.min(jnp.where(own, ecol, 99), axis=1, keepdims=True)
    hi = jnp.max(jnp.where(own, ecol, -1), axis=1, keepdims=True)
    lane = lax.broadcasted_iota(I32, (32, 128), 1)
    idxv[...] = jnp.where(lane == 0, jnp.minimum(lo, 31), jnp.maximum(hi, 0))
    to_smem = pltpu.make_async_copy(idxv, idxs, idx_sem)
    to_smem.start()
    fields = jnp.concatenate(
        [basis_ref[...], images_ref[0], images_ref[1], cell_ref[...] + 1], axis=0
    ).astype(F32)
    for r, hit in ((0, ecol == lo), (1, (ecol == hi) & (hi != lo))):
        got = lax.dot_general(
            jnp.where(hit, 1.0, 0.0), fields, (((1,), (1,)), ((), ())),
            preferred_element_type=F32,
        )
        pay[r, :, 0:14] = got.astype(I32)
    def dcopy(d):
        return pltpu.make_async_remote_copy(
            dens.at[image], dens.at[image], ds_sem.at[d], dr_sem.at[d],
            device_id=zpeer(d), device_id_type=MESH,
        )

    def fcopy(d):
        src = dens.at[lax.rem(z + NZ - d, NZ) * NC + c]
        return pltpu.make_async_remote_copy(
            src, src, fs_sem.at[d], fr_sem.at[d], device_id=sib, device_id_type=MESH
        )

    def lcopy(k):
        return pltpu.make_async_remote_copy(
            lsend.at[k], lrecv.at[k], ls_sem.at[k], lr_sem.at[k],
            device_id=plane(HOME[k]), device_id_type=MESH,
        )

    def acopy(k):
        return pltpu.make_async_remote_copy(
            packa.at[k], recva.at[k], as_sem.at[k], ar_sem.at[k],
            device_id=plane(ALT[k]), device_id_type=MESH,
        )

    def hcopy(k):
        return pltpu.make_async_remote_copy(
            packh.at[k], recvh.at[k], hs_sem.at[k], hr_sem.at[k],
            device_id=plane(HOME[k]), device_id_type=MESH,
        )

    def pack(k, off, shift, buf, local):
        q = row_of(y, x, off[0] + shift, off[1])
        dst = local if k == 0 else buf
        for r in range(2):
            dst[k, r * 64 : (r + 1) * 64, :] = blk[idxs[q, r]]

    for k, o in enumerate(HOME):
        o1, o2 = row_of(y, x, o[0], o[1]), row_of(y, x, o[0] + 4, o[1])
        dst = lrecv if k == 0 else lsend
        for s, (r, q) in enumerate(((0, o1), (1, o1), (0, o2), (1, o2))):
            dst[k, s : s + 1, :] = pay[r, pl.ds(q, 1), :]
    to_smem.wait()
    for cp in loads[4:]:
        cp.wait()
    for k in range(NA):
        pack(k, ALT[k], 4, packa, recva)
    pl.semaphore_wait(bar, len(peers))
    for d in (4, 3, 5, 2, 6, 1, 7):
        dcopy(d).start()
    fcopy(0).start()
    for k in range(1, NH):
        lcopy(k).start()
    for k in range(1, NA):
        acopy(k).start()
    for k in range(NH):
        pack(k, HOME[k], 0, packh, recvh)
    for k in range(1, NH):
        hcopy(k).start()

    rows2 = lax.broadcasted_iota(I32, (64, 256), 0)
    t = lax.rem(lax.broadcasted_iota(I32, (64, 256), 1), 128)
    xmask = ((t < 64) & (lax.rem(t, 8) == lax.div(rows2, 8))) | (
        (t >= 64) & (lax.div(t - 64, 8) == lax.rem(rows2, 8))
    )
    pi = lax.broadcasted_iota(I32, (256, 256), 0)
    pj = lax.broadcasted_iota(I32, (256, 256), 1)
    pt, u = lax.rem(pi, 128), lax.rem(pj, 64)
    same_r = lax.div(pi, 128) == lax.rem(lax.div(pj, 64), 2)
    occ_part = same_r & (pt < 64) & (pj < 128) & (lax.div(pt, 8) == lax.div(u, 8))
    virt_part = same_r & (pt >= 64) & (pj >= 128) & (lax.rem(pt, 8) == lax.rem(u, 8))
    spread = jnp.where(occ_part | virt_part, 1.0, 0.0).astype(BF16)

    for k in range(1, NH):
        lcopy(k).wait_recv()
    for n in range(NPAIR):
        k, s = (HOME.index(ALT[n]), 2) if n < NA else (n - NA, 0)
        for r in range(2):
            lists[r * 32 + n : r * 32 + n + 1, :] = lrecv[k, s + r : s + r + 1, :]
    fr = lists[...]
    low = lax.broadcasted_iota(I32, (32, 128), 1) < 64
    for j in range(4):
        cell = jnp.broadcast_to(fr[:, 10 + j : 11 + j], (64, 128))
        cel[j] = jnp.where(low, cell[0:32], cell[32:64])
    basis = lax.broadcasted_iota(I32, (64, 256), 1)
    pick = jnp.concatenate(
        [
            jnp.where(jnp.broadcast_to(fr[:, f : f + 1], (64, 256)) == basis, 1.0, 0.0)
            for f in range(2)
        ],
        axis=0,
    ).astype(BF16)

    lane64 = lax.broadcasted_iota(I32, (64, 128), 1) < 64
    for j in range(4):
        want[j] = jnp.where(
            lane64,
            jnp.broadcast_to(fr[:, 2 + j : 3 + j], (64, 128)),
            jnp.broadcast_to(fr[:, 6 + j : 7 + j], (64, 128)),
        )
    sel[...] = jnp.zeros_like(sel)

    def choose(d, core):
        img = lax.rem(z + NZ - d, NZ) * NC + core
        v = lax.dot_general(
            pick, dens[img], (((1,), (1,)), ((), ())), preferred_element_type=F32
        )
        v = jnp.where(lane64, v[0:64], v[64:128])
        for j in range(4):
            hit = want[j] == img
            for r in range(2):
                rs, ls = slice(r * 32, (r + 1) * 32), slice(r * 128, (r + 1) * 128)
                sel[j, :, ls] = jnp.where(hit[rs], v[rs], sel[j, :, ls])

    choose(0, c)
    last = 0
    for d in (1, 7, 2, 6, 3, 5, 4):
        dcopy(d).wait_recv()
        fcopy(d).start()
        choose(d, c)
        fcopy(last).wait_recv()
        choose(last, 1 - c)
        last = d
    fcopy(last).wait_recv()
    choose(last, 1 - c)

    def build(n, carry):
        spot = jnp.concatenate(
            [
                jnp.where(xmask, jnp.broadcast_to(sel[j, pl.ds(n, 1), :], (64, 256)), 0.0)
                for j in range(4)
            ],
            axis=0,
        ).astype(BF16)
        e = jnp.dot(spot, spread, preferred_element_type=F32)
        kron = e[:, :128] * e[:, 128:]
        acc = [jnp.zeros((64, 128), F32) for _ in range(4)]
        for j in range(4):
            cell = jnp.broadcast_to(cel[j, pl.ds(n, 1), :], (64, 128))
            for q in range(4):
                acc[q] = acc[q] + jnp.where(cell == q + 1, kron[j * 64 : (j + 1) * 64], 0.0)
        for q in range(4):
            ls = slice(q * 128, (q + 1) * 128)
            ops[n, 0:64, ls] = jnp.where(lane64, acc[q], 0.0).astype(BF16)
            ops[n, 64:128, ls] = jnp.where(lane64, 0.0, acc[q]).astype(BF16)
        return carry

    lax.fori_loop(0, NPAIR, build, 0, unroll=4)

    def group(recv, chi, first, g):
        b = jnp.concatenate([recv[4 * g + i] for i in range(4)], axis=0)
        bt = b.T
        mixed = [
            jnp.dot(
                bt[:, i * 128 : (i + 1) * 128], ops[first + 4 * g + i], preferred_element_type=F32
            ).astype(BF16)
            for i in range(4)
        ]
        for q in range(4):
            m = jnp.concatenate([p[:, q * 128 : (q + 1) * 128] for p in mixed], axis=1)
            chi[q] += jnp.dot(m, b, preferred_element_type=F32)

    def wait_pair(recv, sem, n):
        pltpu.make_async_remote_copy(
            recv.at[n], recv.at[n], sem.at[n], sem.at[n], device_id=sib, device_id_type=MESH
        ).wait_recv()

    def run_groups(recv, sem, chi, first, start, stop):
        def body(g, carry):
            @pl.when(g > 0)
            def _():
                wait_pair(recv, sem, 4 * g)

            for i in range(1, 4):
                wait_pair(recv, sem, 4 * g + i)
            group(recv, chi, first, g)
            return carry

        lax.fori_loop(start, stop, body, 0)

    def scopy(buf, rbuf, w):
        return pltpu.make_async_remote_copy(
            buf, rbuf, s_ssem.at[w], s_rsem.at[w], device_id=sib, device_id_type=MESH
        )

    def zcopy(buf, rbuf, w, d):
        return pltpu.make_async_remote_copy(
            buf.at[d], rbuf.at[d], z_ssem.at[w, d], z_rsem.at[w, d],
            device_id=zpeer(d), device_id_type=MESH,
        )

    def share_rows(d, core):
        zz = lax.rem(z + d, NZ)
        return pl.ds(pl.multiple_of((zz * NC + core) * 16, 16), 16)

    def to_sibling(chi, buf, rbuf, w):
        def body(d, carry):
            buf[d] = chi[:, share_rows(d, 1 - c), :].astype(BF16)
            return carry

        lax.fori_loop(0, NZ, body, 0)
        scopy(buf, rbuf, w).start()

    def to_chips(chi, buf, rbuf, zbuf, w):
        scopy(buf, rbuf, w).wait_recv()

        def body(d, carry):
            zbuf[d] = (chi[:, share_rows(d, c), :] + rbuf[d].astype(F32)).astype(BF16)
            return carry

        lax.fori_loop(1, NZ, body, 0)
        return chi[:, share_rows(0, c), :] + rbuf[0].astype(F32)

    chia[...] = jnp.zeros_like(chia)
    chih[...] = jnp.zeros_like(chih)
    run_groups(recva, ar_sem, chia, 0, 0, NA // 4)
    to_sibling(chia, sa, sra, 0)
    run_groups(recvh, hr_sem, chih, NA, 0, 1)
    out_ref[...] = to_chips(chia, sa, sra, za, 0)
    for d in (4, 3, 5, 2, 6, 1, 7):
        zcopy(za, zra, 0, d).start()
    run_groups(recvh, hr_sem, chih, NA, 1, 3)
    total = out_ref[...]
    for d in range(1, NZ):
        zcopy(za, zra, 0, d).wait_recv()
        total = total + zra[d].astype(F32)
    ex[...] = total.astype(BF16)
    to_far = pltpu.make_async_remote_copy(
        ex, exr, e_ssem, e_rsem, device_id=far, device_id_type=MESH
    )
    to_far.start()
    run_groups(recvh, hr_sem, chih, NA, 3, NH // 4)
    to_sibling(chih, sh, srh, 1)
    mine = to_chips(chih, sh, srh, zh, 1)
    for d in (4, 3, 5, 2, 6, 1, 7):
        zcopy(zh, zrh, 1, d).start()
    to_far.wait_recv()
    mine = mine + exr[...].astype(F32)
    for d in (1, 7, 2, 6, 3, 5, 4):
        zcopy(zh, zrh, 1, d).wait_recv()
        mine = mine + zrh[d].astype(F32)
    out_ref[...] = mine
    result = pltpu.make_async_copy(out_ref, out_hbm, in_sem.at[7])
    result.start()

    for d in range(1, NZ):
        dcopy(d).wait_send()
        zcopy(za, zra, 0, d).wait_send()
        zcopy(zh, zrh, 1, d).wait_send()
    for d in range(NZ):
        fcopy(d).wait_send()
    for k in range(1, NH):
        lcopy(k).wait_send()
        hcopy(k).wait_send()
    for k in range(1, NA):
        acopy(k).wait_send()
    scopy(sa, sra, 0).wait_send()
    scopy(sh, srh, 1).wait_send()
    to_far.wait_send()
    result.wait()


def phase_kernel(lat_ref, cos_ref, chi_ref, out_ref, buf, sem):
    points, parts = KGRID * KGRID, sem.shape[0]
    n = points // parts
    cells = chi_ref.shape[0]
    pieces = [chi_ref[r] for r in range(cells)]
    lat = [(lat_ref[0, r], lat_ref[1, r]) for r in range(cells)]

    def copy(i):
        ks = slice(i * n, (i + 1) * n)
        return pltpu.make_async_copy(buf.at[:, ks], out_ref.at[:, ks], sem.at[i])

    for k in range(points):
        k1, k2 = k // KGRID, k % KGRID
        re = im = None
        for r in range(cells):
            w = (k1 * lat[r][0] + k2 * lat[r][1]) & (KGRID - 1)
            a, b = cos_ref[w] * pieces[r], cos_ref[(w + 6) & (KGRID - 1)] * pieces[r]
            re, im = (a, b) if re is None else (re + a, im + b)
        buf[0, k, 0] = re
        buf[1, k, 0] = im
        if k % n == n - 1:
            copy(k // n).start()
    for i in range(parts):
        copy(i).wait()


def local(blocks, block_owner, block_basis, pair_images, pair_cell, lattice, dens_occ, dens_virt):
    width = blocks.shape[2]
    cells = lattice.shape[0]
    vm = pltpu.VMEM
    dma = pltpu.SemaphoreType.DMA
    share = (NZ, cells, 16, width)
    chi = pl.pallas_call(
        main_kernel,
        out_shape=jax.ShapeDtypeStruct((cells, 16, width), F32),
        in_specs=[pl.BlockSpec(memory_space=pltpu.HBM)] * 7,
        out_specs=pl.BlockSpec(memory_space=pltpu.HBM),
        scratch_shapes=[
            vm((1, 32), I32),
            vm((2, 32), I32),
            vm((2, 4, 32), I32),
            vm((4, 32), I32),
            vm((32, 64, width), BF16),
            vm((cells, 16, width), F32),
            vm((NA, 128, width), BF16),
            vm((NH, 128, width), BF16),
            vm((NA, 128, width), BF16),
            vm((NH, 128, width), BF16),
            vm((NH, 8, 128), I32),
            vm((NH, 8, 128), I32),
            vm((2, 32, 128), I32),
            vm((32, 128), I32),
            pltpu.SMEM((32, 128), I32),
            vm((NZ * NC, 128, 256), BF16),
            vm((4, NPAIR, 256), F32),
            vm((4, 2 * NPAIR, 128), I32),
            vm((4, NPAIR, 128), I32),
            vm((NPAIR, 128, 512), BF16),
            vm((cells, width, width), F32),
            vm((cells, width, width), F32),
        ]
        + [vm(share, BF16)] * 8
        + [vm(share[1:], BF16)] * 2
        + [vm((64, 128), I32)]
        + [
            dma((8,)), dma(()),
            dma((NA,)), dma((NA,)), dma((NH,)), dma((NH,)), dma((NH,)), dma((NH,)),
            dma((NZ,)), dma((NZ,)), dma((NZ,)), dma((NZ,)),
            dma((2,)), dma((2,)), dma((2, NZ)), dma((2, NZ)), dma(()), dma(()),
        ],
        compiler_params=pltpu.CompilerParams(
            collective_id=0, has_side_effects=True, vmem_limit_bytes=60 << 20
        ),
    )(
        block_owner.T, block_basis.T, jnp.transpose(pair_images, (1, 2, 0)), pair_cell.T,
        jnp.swapaxes(dens_occ, 1, 2), jnp.swapaxes(dens_virt, 1, 2), blocks,
    )
    table = jnp.asarray(np.cos(2.0 * math.pi / KGRID * np.arange(KGRID)), F32)
    full = (2, KGRID * KGRID, 1, 16, width)
    return pl.pallas_call(
        phase_kernel,
        out_shape=jax.ShapeDtypeStruct(full, F32),
        in_specs=[
            pl.BlockSpec(memory_space=pltpu.SMEM),
            pl.BlockSpec(memory_space=pltpu.SMEM),
            pl.BlockSpec(memory_space=pltpu.VMEM),
        ],
        out_specs=pl.BlockSpec(memory_space=pl.ANY),
        scratch_shapes=[pltpu.VMEM(full, F32), pltpu.SemaphoreType.DMA((8,))],
    )(lattice.T, table, chi)


def solution(mesh):
    both = ("image", "ri")
    placed = (
        P(both, None, None),
        P(both, None),
        P(both, None),
        P(both, None, None),
        P(both, None),
        P(),
        P("image", None, None),
        P("image", None, None),
    )
    return jax.shard_map(
        local,
        mesh=mesh,
        in_specs=placed,
        out_specs=P(None, None, "ri", "image", None),
        check_vma=False,
    )
```

```python
import functools
import math

import jax
import jax.numpy as jnp
import numpy as np
from jax import lax
from jax.experimental import pallas as pl
from jax.experimental.pallas import tpu as pltpu
from jax.sharding import PartitionSpec as P

KGRID = 8
MESH = pl.DeviceIdType.MESH
NX, NY, NZ, NC = 4, 8, 8, 2
F32, BF16, I32 = jnp.float32, jnp.bfloat16, jnp.int32

ALT = [
    (0, 0), (1, 0), (-1, 0), (0, 1), (0, 3), (1, 1),
    (-1, 3), (1, 3), (-1, 1), (0, 2), (1, 2), (-1, 2),
]
HOME = [
    (0, 0), (1, 0), (-1, 0), (0, 1), (0, 3), (0, 2), (1, 1), (-1, 3), (1, 3), (-1, 1), (2, 0),
    (-2, 0), (1, 2), (-1, 2), (2, 1), (-2, 3), (2, 3), (-2, 1), (2, 2), (-2, 2),
]
NA, NH = len(ALT), len(HOME)
NPAIR = NA + NH


def position():
    i, r = lax.axis_index("image"), lax.axis_index("ri")
    return lax.div(i, NC), lax.rem(i, NC), lax.div(r, NX), lax.rem(r, NX)


def row_of(y, x, dy, dx):
    return lax.rem(y + dy + NY, NY) * NX + lax.rem(x + dx + NX, NX)


def main_kernel(
    owner_hbm, basis_hbm, images_hbm, cell_hbm, occ_hbm, virt_hbm, blocks_hbm, out_hbm,
    owner_ref, basis_ref, images_ref, cell_ref, blk, out_ref,    packa, packh, recva, recvh, lsend, lrecv, pay, idxv, idxs,
    dens, sel, want, cel, ops, chia, chih,
    sa, sra, sh, srh, za, zra, zh, zrh, ex, exr, lists,
    in_sem, idx_sem, as_sem, ar_sem, hs_sem, hr_sem, ls_sem, lr_sem,
    ds_sem, dr_sem, fs_sem, fr_sem,
    s_ssem, s_rsem, z_ssem, z_rsem, e_ssem, e_rsem,
):
    z, c, y, x = position()
    image, ri = lax.axis_index("image"), lax.axis_index("ri")
    sib = {"image": z * NC + (1 - c), "ri": ri}
    far = {"image": image, "ri": row_of(y, x, 4, 0)}

    def plane(off, sign=1):
        return {"image": image, "ri": row_of(y, x, sign * off[0], sign * off[1])}

    def zpeer(d):
        return {"image": lax.rem(z + d, NZ) * NC + c, "ri": ri}

    loads = [
        pltpu.make_async_copy(src, dst, in_sem.at[i])
        for i, (src, dst) in enumerate(
            (
                (owner_hbm, owner_ref),
                (basis_hbm, basis_ref),
                (images_hbm, images_ref),
                (cell_hbm, cell_ref),
                (occ_hbm.at[0], dens.at[image, 0:64]),
                (virt_hbm.at[0], dens.at[image, 64:128]),
                (blocks_hbm, blk),
            )
        )
    ]
    for cp in loads:
        cp.start()

    bar = pltpu.get_barrier_semaphore()
    peers = [plane(o) for o in HOME[1:]] + [zpeer(d) for d in range(1, NZ)] + [sib, far]
    for p in peers:
        pl.semaphore_signal(bar, inc=1, device_id=p, device_id_type=MESH)

    for cp in loads[:4]:
        cp.wait()
    orow = lax.broadcasted_iota(I32, (32, 32), 0)
    ecol = lax.broadcasted_iota(I32, (32, 32), 1)
    own = jnp.broadcast_to(owner_ref[...], (32, 32)) == orow
    lo = jnp.min(jnp.where(own, ecol, 99), axis=1, keepdims=True)
    hi = jnp.max(jnp.where(own, ecol, -1), axis=1, keepdims=True)
    lane = lax.broadcasted_iota(I32, (32, 128), 1)
    idxv[...] = jnp.where(lane == 0, jnp.minimum(lo, 31), jnp.maximum(hi, 0))
    to_smem = pltpu.make_async_copy(idxv, idxs, idx_sem)
    to_smem.start()
    fields = jnp.concatenate(
        [basis_ref[...], images_ref[0], images_ref[1], cell_ref[...] + 1], axis=0
    ).astype(F32)
    for r, hit in ((0, ecol == lo), (1, (ecol == hi) & (hi != lo))):
        got = lax.dot_general(
            jnp.where(hit, 1.0, 0.0), fields, (((1,), (1,)), ((), ())),
            preferred_element_type=F32,
        )
        pay[r, :, 0:14] = got.astype(I32)
    def dcopy(d):
        return pltpu.make_async_remote_copy(
            dens.at[image], dens.at[image], ds_sem.at[d], dr_sem.at[d],
            device_id=zpeer(d), device_id_type=MESH,
        )

    def fcopy(d):
        src = dens.at[lax.rem(z + NZ - d, NZ) * NC + c]
        return pltpu.make_async_remote_copy(
            src, src, fs_sem.at[d], fr_sem.at[d], device_id=sib, device_id_type=MESH
        )

    def lcopy(k):
        return pltpu.make_async_remote_copy(
            lsend.at[k], lrecv.at[k], ls_sem.at[k], lr_sem.at[k],
            device_id=plane(HOME[k]), device_id_type=MESH,
        )

    def acopy(k):
        return pltpu.make_async_remote_copy(
            packa.at[k], recva.at[k], as_sem.at[k], ar_sem.at[k],
            device_id=plane(ALT[k]), device_id_type=MESH,
        )

    def hcopy(k):
        return pltpu.make_async_remote_copy(
            packh.at[k], recvh.at[k], hs_sem.at[k], hr_sem.at[k],
            device_id=plane(HOME[k]), device_id_type=MESH,
        )

    def pack(k, off, shift, buf, local):
        q = row_of(y, x, off[0] + shift, off[1])
        dst = local if k == 0 else buf
        for r in range(2):
            dst[k, r * 64 : (r + 1) * 64, :] = blk[idxs[q, r]]

    for k, o in enumerate(HOME):
        o1, o2 = row_of(y, x, o[0], o[1]), row_of(y, x, o[0] + 4, o[1])
        dst = lrecv if k == 0 else lsend
        for s, (r, q) in enumerate(((0, o1), (1, o1), (0, o2), (1, o2))):
            dst[k, s : s + 1, :] = pay[r, pl.ds(q, 1), :]
    to_smem.wait()
    for cp in loads[4:]:
        cp.wait()
    for k in range(NA):
        pack(k, ALT[k], 4, packa, recva)
    pl.semaphore_wait(bar, len(peers))
    for d in (4, 3, 5, 2, 6, 1, 7):
        dcopy(d).start()
    fcopy(0).start()
    for k in range(1, NH):
        lcopy(k).start()
    for k in range(1, NA):
        acopy(k).start()
    for k in range(NH):
        pack(k, HOME[k], 0, packh, recvh)
    for k in range(1, NH):
        hcopy(k).start()

    rows2 = lax.broadcasted_iota(I32, (64, 256), 0)
    t = lax.rem(lax.broadcasted_iota(I32, (64, 256), 1), 128)
    xmask = ((t < 64) & (lax.rem(t, 8) == lax.div(rows2, 8))) | (
        (t >= 64) & (lax.div(t - 64, 8) == lax.rem(rows2, 8))
    )
    pi = lax.broadcasted_iota(I32, (256, 256), 0)
    pj = lax.broadcasted_iota(I32, (256, 256), 1)
    pt, u = lax.rem(pi, 128), lax.rem(pj, 64)
    same_r = lax.div(pi, 128) == lax.rem(lax.div(pj, 64), 2)
    occ_part = same_r & (pt < 64) & (pj < 128) & (lax.div(pt, 8) == lax.div(u, 8))
    virt_part = same_r & (pt >= 64) & (pj >= 128) & (lax.rem(pt, 8) == lax.rem(u, 8))
    spread = jnp.where(occ_part | virt_part, 1.0, 0.0).astype(BF16)

    for k in range(1, NH):
        lcopy(k).wait_recv()
    for n in range(NPAIR):
        k, s = (HOME.index(ALT[n]), 2) if n < NA else (n - NA, 0)
        for r in range(2):
            lists[r * 32 + n : r * 32 + n + 1, :] = lrecv[k, s + r : s + r + 1, :]
    fr = lists[...]
    low = lax.broadcasted_iota(I32, (32, 128), 1) < 64
    for j in range(4):
        cell = jnp.broadcast_to(fr[:, 10 + j : 11 + j], (64, 128))
        cel[j] = jnp.where(low, cell[0:32], cell[32:64])
    basis = lax.broadcasted_iota(I32, (64, 256), 1)
    pick = jnp.concatenate(
        [
            jnp.where(jnp.broadcast_to(fr[:, f : f + 1], (64, 256)) == basis, 1.0, 0.0)
            for f in range(2)
        ],
        axis=0,
    ).astype(BF16)

    lane64 = lax.broadcasted_iota(I32, (64, 128), 1) < 64
    for j in range(4):
        want[j] = jnp.where(
            lane64,
            jnp.broadcast_to(fr[:, 2 + j : 3 + j], (64, 128)),
            jnp.broadcast_to(fr[:, 6 + j : 7 + j], (64, 128)),
        )
    sel[...] = jnp.zeros_like(sel)

    def choose(d, core):
        img = lax.rem(z + NZ - d, NZ) * NC + core
        v = lax.dot_general(
            pick, dens[img], (((1,), (1,)), ((), ())), preferred_element_type=F32
        )
        v = jnp.where(lane64, v[0:64], v[64:128])
        for j in range(4):
            hit = want[j] == img
            for r in range(2):
                rs, ls = slice(r * 32, (r + 1) * 32), slice(r * 128, (r + 1) * 128)
                sel[j, :, ls] = jnp.where(hit[rs], v[rs], sel[j, :, ls])

    choose(0, c)
    last = 0
    for d in (1, 7, 2, 6, 3, 5, 4):
        dcopy(d).wait_recv()
        fcopy(d).start()
        choose(d, c)
        fcopy(last).wait_recv()
        choose(last, 1 - c)
        last = d
    fcopy(last).wait_recv()
    choose(last, 1 - c)

    def build(n, carry):
        spot = jnp.concatenate(
            [
                jnp.where(xmask, jnp.broadcast_to(sel[j, pl.ds(n, 1), :], (64, 256)), 0.0)
                for j in range(4)
            ],
            axis=0,
        ).astype(BF16)
        e = jnp.dot(spot, spread, preferred_element_type=F32)
        kron = e[:, :128] * e[:, 128:]
        acc = [jnp.zeros((64, 128), F32) for _ in range(4)]
        for j in range(4):
            cell = jnp.broadcast_to(cel[j, pl.ds(n, 1), :], (64, 128))
            for q in range(4):
                acc[q] = acc[q] + jnp.where(cell == q + 1, kron[j * 64 : (j + 1) * 64], 0.0)
        for q in range(4):
            ls = slice(q * 128, (q + 1) * 128)
            ops[n, 0:64, ls] = jnp.where(lane64, acc[q], 0.0).astype(BF16)
            ops[n, 64:128, ls] = jnp.where(lane64, 0.0, acc[q]).astype(BF16)
        return carry

    lax.fori_loop(0, NPAIR, build, 0, unroll=4)

    def group(recv, chi, first, g):
        b = jnp.concatenate([recv[4 * g + i] for i in range(4)], axis=0)
        bt = b.T
        mixed = [
            jnp.dot(
                bt[:, i * 128 : (i + 1) * 128], ops[first + 4 * g + i], preferred_element_type=F32
            ).astype(BF16)
            for i in range(4)
        ]
        for q in range(4):
            m = jnp.concatenate([p[:, q * 128 : (q + 1) * 128] for p in mixed], axis=1)
            chi[q] += jnp.dot(m, b, preferred_element_type=F32)

    def wait_pair(recv, sem, n):
        pltpu.make_async_remote_copy(
            recv.at[n], recv.at[n], sem.at[n], sem.at[n], device_id=sib, device_id_type=MESH
        ).wait_recv()

    def run_groups(recv, sem, chi, first, start, stop):
        def body(g, carry):
            @pl.when(g > 0)
            def _():
                wait_pair(recv, sem, 4 * g)

            for i in range(1, 4):
                wait_pair(recv, sem, 4 * g + i)
            group(recv, chi, first, g)
            return carry

        lax.fori_loop(start, stop, body, 0)

    def scopy(buf, rbuf, w):
        return pltpu.make_async_remote_copy(
            buf, rbuf, s_ssem.at[w], s_rsem.at[w], device_id=sib, device_id_type=MESH
        )

    def zcopy(buf, rbuf, w, d):
        return pltpu.make_async_remote_copy(
            buf.at[d], rbuf.at[d], z_ssem.at[w, d], z_rsem.at[w, d],
            device_id=zpeer(d), device_id_type=MESH,
        )

    def share_rows(d, core):
        zz = lax.rem(z + d, NZ)
        return pl.ds(pl.multiple_of((zz * NC + core) * 16, 16), 16)

    def to_sibling(chi, buf, rbuf, w):
        def body(d, carry):
            buf[d] = chi[:, share_rows(d, 1 - c), :].astype(BF16)
            return carry

        lax.fori_loop(0, NZ, body, 0)
        scopy(buf, rbuf, w).start()

    def to_chips(chi, buf, rbuf, zbuf, w):
        scopy(buf, rbuf, w).wait_recv()

        def body(d, carry):
            zbuf[d] = (chi[:, share_rows(d, c), :] + rbuf[d].astype(F32)).astype(BF16)
            return carry

        lax.fori_loop(1, NZ, body, 0)
        return chi[:, share_rows(0, c), :] + rbuf[0].astype(F32)

    chia[...] = jnp.zeros_like(chia)
    chih[...] = jnp.zeros_like(chih)
    run_groups(recva, ar_sem, chia, 0, 0, NA // 4)
    to_sibling(chia, sa, sra, 0)
    out_ref[...] = to_chips(chia, sa, sra, za, 0)
    for d in (4, 3, 5, 2, 6, 1, 7):
        zcopy(za, zra, 0, d).start()
    run_groups(recvh, hr_sem, chih, NA, 0, 1)
    run_groups(recvh, hr_sem, chih, NA, 1, 3)
    total = out_ref[...]
    for d in range(1, NZ):
        zcopy(za, zra, 0, d).wait_recv()
        total = total + zra[d].astype(F32)
    ex[...] = total.astype(BF16)
    to_far = pltpu.make_async_remote_copy(
        ex, exr, e_ssem, e_rsem, device_id=far, device_id_type=MESH
    )
    to_far.start()
    run_groups(recvh, hr_sem, chih, NA, 3, NH // 4)
    to_sibling(chih, sh, srh, 1)
    mine = to_chips(chih, sh, srh, zh, 1)
    for d in (4, 3, 5, 2, 6, 1, 7):
        zcopy(zh, zrh, 1, d).start()
    to_far.wait_recv()
    mine = mine + exr[...].astype(F32)
    for d in (1, 7, 2, 6, 3, 5, 4):
        zcopy(zh, zrh, 1, d).wait_recv()
        mine = mine + zrh[d].astype(F32)
    out_ref[...] = mine
    result = pltpu.make_async_copy(out_ref, out_hbm, in_sem.at[7])
    result.start()

    for d in range(1, NZ):
        dcopy(d).wait_send()
        zcopy(za, zra, 0, d).wait_send()
        zcopy(zh, zrh, 1, d).wait_send()
    for d in range(NZ):
        fcopy(d).wait_send()
    for k in range(1, NH):
        lcopy(k).wait_send()
        hcopy(k).wait_send()
    for k in range(1, NA):
        acopy(k).wait_send()
    scopy(sa, sra, 0).wait_send()
    scopy(sh, srh, 1).wait_send()
    to_far.wait_send()
    result.wait()


def phase_kernel(lat_ref, cos_ref, chi_ref, out_ref, buf, sem):
    points, parts = KGRID * KGRID, sem.shape[0]
    n = points // parts
    cells = chi_ref.shape[0]
    pieces = [chi_ref[r] for r in range(cells)]
    lat = [(lat_ref[0, r], lat_ref[1, r]) for r in range(cells)]

    def copy(i):
        ks = slice(i * n, (i + 1) * n)
        return pltpu.make_async_copy(buf.at[:, ks], out_ref.at[:, ks], sem.at[i])

    for k in range(points):
        k1, k2 = k // KGRID, k % KGRID
        re = im = None
        for r in range(cells):
            w = (k1 * lat[r][0] + k2 * lat[r][1]) & (KGRID - 1)
            a, b = cos_ref[w] * pieces[r], cos_ref[(w + 6) & (KGRID - 1)] * pieces[r]
            re, im = (a, b) if re is None else (re + a, im + b)
        buf[0, k, 0] = re
        buf[1, k, 0] = im
        if k % n == n - 1:
            copy(k // n).start()
    for i in range(parts):
        copy(i).wait()


def local(blocks, block_owner, block_basis, pair_images, pair_cell, lattice, dens_occ, dens_virt):
    width = blocks.shape[2]
    cells = lattice.shape[0]
    vm = pltpu.VMEM
    dma = pltpu.SemaphoreType.DMA
    share = (NZ, cells, 16, width)
    chi = pl.pallas_call(
        main_kernel,
        out_shape=jax.ShapeDtypeStruct((cells, 16, width), F32),
        in_specs=[pl.BlockSpec(memory_space=pltpu.HBM)] * 7,
        out_specs=pl.BlockSpec(memory_space=pltpu.HBM),
        scratch_shapes=[
            vm((1, 32), I32),
            vm((2, 32), I32),
            vm((2, 4, 32), I32),
            vm((4, 32), I32),
            vm((32, 64, width), BF16),
            vm((cells, 16, width), F32),
            vm((NA, 128, width), BF16),
            vm((NH, 128, width), BF16),
            vm((NA, 128, width), BF16),
            vm((NH, 128, width), BF16),
            vm((NH, 8, 128), I32),
            vm((NH, 8, 128), I32),
            vm((2, 32, 128), I32),
            vm((32, 128), I32),
            pltpu.SMEM((32, 128), I32),
            vm((NZ * NC, 128, 256), BF16),
            vm((4, NPAIR, 256), F32),
            vm((4, 2 * NPAIR, 128), I32),
            vm((4, NPAIR, 128), I32),
            vm((NPAIR, 128, 512), BF16),
            vm((cells, width, width), F32),
            vm((cells, width, width), F32),
        ]
        + [vm(share, BF16)] * 8
        + [vm(share[1:], BF16)] * 2
        + [vm((64, 128), I32)]
        + [
            dma((8,)), dma(()),
            dma((NA,)), dma((NA,)), dma((NH,)), dma((NH,)), dma((NH,)), dma((NH,)),
            dma((NZ,)), dma((NZ,)), dma((NZ,)), dma((NZ,)),
            dma((2,)), dma((2,)), dma((2, NZ)), dma((2, NZ)), dma(()), dma(()),
        ],
        compiler_params=pltpu.CompilerParams(
            collective_id=0, has_side_effects=True, vmem_limit_bytes=60 << 20
        ),
    )(
        block_owner.T, block_basis.T, jnp.transpose(pair_images, (1, 2, 0)), pair_cell.T,
        jnp.swapaxes(dens_occ, 1, 2), jnp.swapaxes(dens_virt, 1, 2), blocks,
    )
    table = jnp.asarray(np.cos(2.0 * math.pi / KGRID * np.arange(KGRID)), F32)
    full = (2, KGRID * KGRID, 1, 16, width)
    return pl.pallas_call(
        phase_kernel,
        out_shape=jax.ShapeDtypeStruct(full, F32),
        in_specs=[
            pl.BlockSpec(memory_space=pltpu.SMEM),
            pl.BlockSpec(memory_space=pltpu.SMEM),
            pl.BlockSpec(memory_space=pltpu.VMEM),
        ],
        out_specs=pl.BlockSpec(memory_space=pl.ANY),
        scratch_shapes=[pltpu.VMEM(full, F32), pltpu.SemaphoreType.DMA((8,))],
    )(lattice.T, table, chi)


def solution(mesh):
    both = ("image", "ri")
    placed = (
        P(both, None, None),
        P(both, None),
        P(both, None),
        P(both, None, None),
        P(both, None),
        P(),
        P("image", None, None),
        P("image", None, None),
    )
    return jax.shard_map(
        local,
        mesh=mesh,
        in_specs=placed,
        out_specs=P(None, None, "ri", "image", None),
        check_vma=False,
    )
```

```python
import functools
import math

import jax
import jax.numpy as jnp
import numpy as np
from jax import lax
from jax.experimental import pallas as pl
from jax.experimental.pallas import tpu as pltpu
from jax.sharding import PartitionSpec as P

KGRID = 8
MESH = pl.DeviceIdType.MESH
NX, NY, NZ, NC = 4, 8, 8, 2
F32, BF16, I32 = jnp.float32, jnp.bfloat16, jnp.int32

ALT = [
    (0, 0), (1, 0), (-1, 0), (0, 1), (0, 3), (1, 1),
    (-1, 3), (1, 3), (-1, 1), (0, 2), (1, 2), (-1, 2),
]
HOME = [
    (0, 0), (1, 0), (-1, 0), (0, 1), (0, 3), (0, 2), (1, 1), (-1, 3), (1, 3), (-1, 1), (2, 0),
    (-2, 0), (1, 2), (-1, 2), (2, 1), (-2, 3), (2, 3), (-2, 1), (2, 2), (-2, 2),
]
NA, NH = len(ALT), len(HOME)
NPAIR = NA + NH


def position():
    i, r = lax.axis_index("image"), lax.axis_index("ri")
    return lax.div(i, NC), lax.rem(i, NC), lax.div(r, NX), lax.rem(r, NX)


def row_of(y, x, dy, dx):
    return lax.rem(y + dy + NY, NY) * NX + lax.rem(x + dx + NX, NX)


def main_kernel(
    owner_hbm, basis_hbm, images_hbm, cell_hbm, occ_hbm, virt_hbm, blocks_hbm, out_hbm,
    owner_ref, basis_ref, images_ref, cell_ref, blk, out_ref,    packa, packh, recva, recvh, lsend, lrecv, pay, idxv, idxs,
    dens, sel, want, cel, ops, chia, chih,
    sa, sra, sh, srh, za, zra, zh, zrh, ex, exr, lists,
    in_sem, idx_sem, as_sem, ar_sem, hs_sem, hr_sem, ls_sem, lr_sem,
    ds_sem, dr_sem, fs_sem, fr_sem,
    s_ssem, s_rsem, z_ssem, z_rsem, e_ssem, e_rsem,
):
    z, c, y, x = position()
    image, ri = lax.axis_index("image"), lax.axis_index("ri")
    sib = {"image": z * NC + (1 - c), "ri": ri}
    far = {"image": image, "ri": row_of(y, x, 4, 0)}

    def plane(off, sign=1):
        return {"image": image, "ri": row_of(y, x, sign * off[0], sign * off[1])}

    def zpeer(d):
        return {"image": lax.rem(z + d, NZ) * NC + c, "ri": ri}

    loads = [
        pltpu.make_async_copy(src, dst, in_sem.at[i])
        for i, (src, dst) in enumerate(
            (
                (owner_hbm, owner_ref),
                (basis_hbm, basis_ref),
                (images_hbm, images_ref),
                (cell_hbm, cell_ref),
                (occ_hbm.at[0], dens.at[image, 0:64]),
                (virt_hbm.at[0], dens.at[image, 64:128]),
                (blocks_hbm, blk),
            )
        )
    ]
    for cp in loads:
        cp.start()

    bar = pltpu.get_barrier_semaphore()
    peers = [plane(o) for o in HOME[1:]] + [zpeer(d) for d in range(1, NZ)] + [sib, far]
    for p in peers:
        pl.semaphore_signal(bar, inc=1, device_id=p, device_id_type=MESH)

    for cp in loads[:4]:
        cp.wait()
    orow = lax.broadcasted_iota(I32, (32, 32), 0)
    ecol = lax.broadcasted_iota(I32, (32, 32), 1)
    own = jnp.broadcast_to(owner_ref[...], (32, 32)) == orow
    lo = jnp.min(jnp.where(own, ecol, 99), axis=1, keepdims=True)
    hi = jnp.max(jnp.where(own, ecol, -1), axis=1, keepdims=True)
    lane = lax.broadcasted_iota(I32, (32, 128), 1)
    idxv[...] = jnp.where(lane == 0, jnp.minimum(lo, 31), jnp.maximum(hi, 0))
    to_smem = pltpu.make_async_copy(idxv, idxs, idx_sem)
    to_smem.start()
    fields = jnp.concatenate(
        [basis_ref[...], images_ref[0], images_ref[1], cell_ref[...] + 1], axis=0
    ).astype(F32)
    for r, hit in ((0, ecol == lo), (1, (ecol == hi) & (hi != lo))):
        got = lax.dot_general(
            jnp.where(hit, 1.0, 0.0), fields, (((1,), (1,)), ((), ())),
            preferred_element_type=F32,
        )
        pay[r, :, 0:14] = got.astype(I32)
    def dcopy(d):
        return pltpu.make_async_remote_copy(
            dens.at[image], dens.at[image], ds_sem.at[d], dr_sem.at[d],
            device_id=zpeer(d), device_id_type=MESH,
        )

    def fcopy(d):
        src = dens.at[lax.rem(z + NZ - d, NZ) * NC + c]
        return pltpu.make_async_remote_copy(
            src, src, fs_sem.at[d], fr_sem.at[d], device_id=sib, device_id_type=MESH
        )

    def lcopy(k):
        return pltpu.make_async_remote_copy(
            lsend.at[k], lrecv.at[k], ls_sem.at[k], lr_sem.at[k],
            device_id=plane(HOME[k]), device_id_type=MESH,
        )

    def acopy(k):
        return pltpu.make_async_remote_copy(
            packa.at[k], recva.at[k], as_sem.at[k], ar_sem.at[k],
            device_id=plane(ALT[k]), device_id_type=MESH,
        )

    def hcopy(k):
        return pltpu.make_async_remote_copy(
            packh.at[k], recvh.at[k], hs_sem.at[k], hr_sem.at[k],
            device_id=plane(HOME[k]), device_id_type=MESH,
        )

    def pack(k, off, shift, buf, local):
        q = row_of(y, x, off[0] + shift, off[1])
        dst = local if k == 0 else buf
        for r in range(2):
            dst[k, r * 64 : (r + 1) * 64, :] = blk[idxs[q, r]]

    for k, o in enumerate(HOME):
        o1, o2 = row_of(y, x, o[0], o[1]), row_of(y, x, o[0] + 4, o[1])
        dst = lrecv if k == 0 else lsend
        for s, (r, q) in enumerate(((0, o1), (1, o1), (0, o2), (1, o2))):
            dst[k, s : s + 1, :] = pay[r, pl.ds(q, 1), :]
    to_smem.wait()
    for cp in loads[4:]:
        cp.wait()
    for k in range(NA):
        pack(k, ALT[k], 4, packa, recva)
    pl.semaphore_wait(bar, len(peers))
    for d in (4, 3, 5, 2, 6, 1, 7):
        dcopy(d).start()
    fcopy(0).start()
    for k in range(1, NH):
        lcopy(k).start()
    for k in range(1, NA):
        acopy(k).start()
    for k in range(NH):
        pack(k, HOME[k], 0, packh, recvh)
    for k in range(1, NH):
        hcopy(k).start()

    rows2 = lax.broadcasted_iota(I32, (64, 256), 0)
    t = lax.rem(lax.broadcasted_iota(I32, (64, 256), 1), 128)
    xmask = ((t < 64) & (lax.rem(t, 8) == lax.div(rows2, 8))) | (
        (t >= 64) & (lax.div(t - 64, 8) == lax.rem(rows2, 8))
    )
    pi = lax.broadcasted_iota(I32, (256, 256), 0)
    pj = lax.broadcasted_iota(I32, (256, 256), 1)
    pt, u = lax.rem(pi, 128), lax.rem(pj, 64)
    same_r = lax.div(pi, 128) == lax.rem(lax.div(pj, 64), 2)
    occ_part = same_r & (pt < 64) & (pj < 128) & (lax.div(pt, 8) == lax.div(u, 8))
    virt_part = same_r & (pt >= 64) & (pj >= 128) & (lax.rem(pt, 8) == lax.rem(u, 8))
    spread = jnp.where(occ_part | virt_part, 1.0, 0.0).astype(BF16)

    for k in range(1, NH):
        lcopy(k).wait_recv()
    for n in range(NPAIR):
        k, s = (HOME.index(ALT[n]), 2) if n < NA else (n - NA, 0)
        for r in range(2):
            lists[r * 32 + n : r * 32 + n + 1, :] = lrecv[k, s + r : s + r + 1, :]
    fr = lists[...]
    low = lax.broadcasted_iota(I32, (32, 128), 1) < 64
    for j in range(4):
        cell = jnp.broadcast_to(fr[:, 10 + j : 11 + j], (64, 128))
        cel[j] = jnp.where(low, cell[0:32], cell[32:64])
    basis = lax.broadcasted_iota(I32, (64, 256), 1)
    pick = jnp.concatenate(
        [
            jnp.where(jnp.broadcast_to(fr[:, f : f + 1], (64, 256)) == basis, 1.0, 0.0)
            for f in range(2)
        ],
        axis=0,
    ).astype(BF16)

    lane64 = lax.broadcasted_iota(I32, (64, 128), 1) < 64
    for j in range(4):
        want[j] = jnp.where(
            lane64,
            jnp.broadcast_to(fr[:, 2 + j : 3 + j], (64, 128)),
            jnp.broadcast_to(fr[:, 6 + j : 7 + j], (64, 128)),
        )
    sel[...] = jnp.zeros_like(sel)

    def choose(d, core):
        img = lax.rem(z + NZ - d, NZ) * NC + core
        v = lax.dot_general(
            pick, dens[img], (((1,), (1,)), ((), ())), preferred_element_type=F32
        )
        v = jnp.where(lane64, v[0:64], v[64:128])
        for j in range(4):
            hit = want[j] == img
            for r in range(2):
                rs, ls = slice(r * 32, (r + 1) * 32), slice(r * 128, (r + 1) * 128)
                sel[j, :, ls] = jnp.where(hit[rs], v[rs], sel[j, :, ls])

    choose(0, c)
    last = 0
    for d in (1, 7, 2, 6, 3, 5, 4):
        dcopy(d).wait_recv()
        fcopy(d).start()
        choose(d, c)
        fcopy(last).wait_recv()
        choose(last, 1 - c)
        last = d
    fcopy(last).wait_recv()
    choose(last, 1 - c)

    def build(n, carry):
        spot = jnp.concatenate(
            [
                jnp.where(xmask, jnp.broadcast_to(sel[j, pl.ds(n, 1), :], (64, 256)), 0.0)
                for j in range(4)
            ],
            axis=0,
        ).astype(BF16)
        e = jnp.dot(spot, spread, preferred_element_type=F32)
        kron = e[:, :128] * e[:, 128:]
        acc = [jnp.zeros((64, 128), F32) for _ in range(4)]
        for j in range(4):
            cell = jnp.broadcast_to(cel[j, pl.ds(n, 1), :], (64, 128))
            for q in range(4):
                acc[q] = acc[q] + jnp.where(cell == q + 1, kron[j * 64 : (j + 1) * 64], 0.0)
        for q in range(4):
            ls = slice(q * 128, (q + 1) * 128)
            ops[n, 0:64, ls] = jnp.where(lane64, acc[q], 0.0).astype(BF16)
            ops[n, 64:128, ls] = jnp.where(lane64, 0.0, acc[q]).astype(BF16)
        return carry

    lax.fori_loop(0, NPAIR, build, 0, unroll=4)

    def group(recv, chi, first, g):
        b = jnp.concatenate([recv[4 * g + i] for i in range(4)], axis=0)
        bt = b.T
        mixed = [
            jnp.dot(
                bt[:, i * 128 : (i + 1) * 128], ops[first + 4 * g + i], preferred_element_type=F32
            ).astype(BF16)
            for i in range(4)
        ]
        for q in range(4):
            m = jnp.concatenate([p[:, q * 128 : (q + 1) * 128] for p in mixed], axis=1)
            chi[q] += jnp.dot(m, b, preferred_element_type=F32)

    def wait_pair(recv, sem, n):
        pltpu.make_async_remote_copy(
            recv.at[n], recv.at[n], sem.at[n], sem.at[n], device_id=sib, device_id_type=MESH
        ).wait_recv()

    def run_groups(recv, sem, chi, first, start, stop):
        def body(g, carry):
            @pl.when(g > 0)
            def _():
                wait_pair(recv, sem, 4 * g)

            for i in range(1, 4):
                wait_pair(recv, sem, 4 * g + i)
            group(recv, chi, first, g)
            return carry

        lax.fori_loop(start, stop, body, 0)

    def scopy(buf, rbuf, w):
        return pltpu.make_async_remote_copy(
            buf, rbuf, s_ssem.at[w], s_rsem.at[w], device_id=sib, device_id_type=MESH
        )

    def zcopy(buf, rbuf, w, d):
        return pltpu.make_async_remote_copy(
            buf.at[d], rbuf.at[d], z_ssem.at[w, d], z_rsem.at[w, d],
            device_id=zpeer(d), device_id_type=MESH,
        )

    def share_rows(d, core):
        zz = lax.rem(z + d, NZ)
        return pl.ds(pl.multiple_of((zz * NC + core) * 16, 16), 16)

    def to_sibling(chi, buf, rbuf, w):
        def body(d, carry):
            buf[d] = chi[:, share_rows(d, 1 - c), :].astype(BF16)
            return carry

        lax.fori_loop(0, NZ, body, 0)
        scopy(buf, rbuf, w).start()

    def to_chips(chi, buf, rbuf, zbuf, w):
        scopy(buf, rbuf, w).wait_recv()

        def body(d, carry):
            zbuf[d] = (chi[:, share_rows(d, c), :] + rbuf[d].astype(F32)).astype(BF16)
            return carry

        lax.fori_loop(1, NZ, body, 0)
        return chi[:, share_rows(0, c), :] + rbuf[0].astype(F32)

    chia[...] = jnp.zeros_like(chia)
    chih[...] = jnp.zeros_like(chih)
    run_groups(recva, ar_sem, chia, 0, 0, NA // 4)
    to_sibling(chia, sa, sra, 0)
    out_ref[...] = to_chips(chia, sa, sra, za, 0)
    for d in (4, 3, 5, 2, 6, 1, 7):
        zcopy(za, zra, 0, d).start()
    run_groups(recvh, hr_sem, chih, NA, 0, 1)
    run_groups(recvh, hr_sem, chih, NA, 1, 3)
    total = out_ref[...]
    for d in range(1, NZ):
        zcopy(za, zra, 0, d).wait_recv()
        total = total + zra[d].astype(F32)
    ex[...] = total.astype(BF16)
    to_far = pltpu.make_async_remote_copy(
        ex, exr, e_ssem, e_rsem, device_id=far, device_id_type=MESH
    )
    to_far.start()
    run_groups(recvh, hr_sem, chih, NA, 3, NH // 4)
    to_sibling(chih, sh, srh, 1)
    mine = to_chips(chih, sh, srh, zh, 1)
    for d in (4, 3, 5, 2, 6, 1, 7):
        zcopy(zh, zrh, 1, d).start()
    to_far.wait_recv()
    mine = mine + exr[...].astype(F32)
    for d in (1, 7, 2, 6, 3, 5, 4):
        zcopy(zh, zrh, 1, d).wait_recv()
        mine = mine + zrh[d].astype(F32)
    out_ref[...] = mine
    result = pltpu.make_async_copy(out_ref, out_hbm, in_sem.at[7])
    result.start()

    for d in range(1, NZ):
        dcopy(d).wait_send()
        zcopy(za, zra, 0, d).wait_send()
        zcopy(zh, zrh, 1, d).wait_send()
    for d in range(NZ):
        fcopy(d).wait_send()
    for k in range(1, NH):
        lcopy(k).wait_send()
        hcopy(k).wait_send()
    for k in range(1, NA):
        acopy(k).wait_send()
    scopy(sa, sra, 0).wait_send()
    scopy(sh, srh, 1).wait_send()
    to_far.wait_send()
    result.wait()


def phase_kernel(lat_ref, cos_ref, chi_ref, out_ref, buf, sem):
    points, parts = KGRID * KGRID, sem.shape[0]
    n = points // parts
    cells = chi_ref.shape[0]
    pieces = [chi_ref[r] for r in range(cells)]
    lat = [(lat_ref[0, r], lat_ref[1, r]) for r in range(cells)]

    def copy(i):
        ks = slice(i * n, (i + 1) * n)
        return pltpu.make_async_copy(buf.at[:, ks], out_ref.at[:, ks], sem.at[i])

    for k in range(points):
        k1, k2 = k // KGRID, k % KGRID
        re = im = None
        for r in range(cells):
            w = (k1 * lat[r][0] + k2 * lat[r][1]) & (KGRID - 1)
            a, b = cos_ref[w] * pieces[r], cos_ref[(w + 6) & (KGRID - 1)] * pieces[r]
            re, im = (a, b) if re is None else (re + a, im + b)
        buf[0, k, 0] = re
        buf[1, k, 0] = im
        if k % n == n - 1:
            copy(k // n).start()
    for i in range(parts):
        copy(i).wait()


def local(blocks, block_owner, block_basis, pair_images, pair_cell, lattice, dens_occ, dens_virt):
    width = blocks.shape[2]
    cells = lattice.shape[0]
    vm = pltpu.VMEM
    dma = pltpu.SemaphoreType.DMA
    share = (NZ, cells, 16, width)
    chi = pl.pallas_call(
        main_kernel,
        out_shape=jax.ShapeDtypeStruct((cells, 16, width), F32),
        in_specs=[pl.BlockSpec(memory_space=pltpu.HBM)] * 7,
        out_specs=pl.BlockSpec(memory_space=pltpu.HBM),
        scratch_shapes=[
            vm((1, 32), I32),
            vm((2, 32), I32),
            vm((2, 4, 32), I32),
            vm((4, 32), I32),
            vm((32, 64, width), BF16),
            vm((cells, 16, width), F32),
            vm((NA, 128, width), BF16),
            vm((NH, 128, width), BF16),
            vm((NA, 128, width), BF16),
            vm((NH, 128, width), BF16),
            vm((NH, 8, 128), I32),
            vm((NH, 8, 128), I32),
            vm((2, 32, 128), I32),
            vm((32, 128), I32),
            pltpu.SMEM((32, 128), I32),
            vm((NZ * NC, 128, 256), BF16),
            vm((4, NPAIR, 256), F32),
            vm((4, 2 * NPAIR, 128), I32),
            vm((4, NPAIR, 128), I32),
            vm((NPAIR, 128, 512), BF16),
            vm((cells, width, width), F32),
            vm((cells, width, width), F32),
        ]
        + [vm(share, BF16)] * 8
        + [vm(share[1:], BF16)] * 2
        + [vm((64, 128), I32)]
        + [
            dma((8,)), dma(()),
            dma((NA,)), dma((NA,)), dma((NH,)), dma((NH,)), dma((NH,)), dma((NH,)),
            dma((NZ,)), dma((NZ,)), dma((NZ,)), dma((NZ,)),
            dma((2,)), dma((2,)), dma((2, NZ)), dma((2, NZ)), dma(()), dma(()),
        ],
        compiler_params=pltpu.CompilerParams(
            collective_id=0, has_side_effects=True, vmem_limit_bytes=60 << 20
        ),
    )(
        block_owner.T, block_basis.T, jnp.transpose(pair_images, (1, 2, 0)), pair_cell.T,
        jnp.swapaxes(dens_occ, 1, 2), jnp.swapaxes(dens_virt, 1, 2), blocks,
    )
    table = jnp.asarray(np.cos(2.0 * math.pi / KGRID * np.arange(KGRID)), F32)
    full = (2, KGRID * KGRID, 1, 16, width)
    return pl.pallas_call(
        phase_kernel,
        out_shape=jax.ShapeDtypeStruct(full, F32),
        in_specs=[
            pl.BlockSpec(memory_space=pltpu.SMEM),
            pl.BlockSpec(memory_space=pltpu.SMEM),
            pl.BlockSpec(memory_space=pltpu.VMEM),
        ],
        out_specs=pl.BlockSpec(memory_space=pl.ANY),
        scratch_shapes=[pltpu.VMEM(full, F32), pltpu.SemaphoreType.DMA((16,))],
    )(lattice.T, table, chi)


def solution(mesh):
    both = ("image", "ri")
    placed = (
        P(both, None, None),
        P(both, None),
        P(both, None),
        P(both, None, None),
        P(both, None),
        P(),
        P("image", None, None),
        P("image", None, None),
    )
    return jax.shard_map(
        local,
        mesh=mesh,
        in_specs=placed,
        out_specs=P(None, None, "ri", "image", None),
        check_vma=False,
    )
```
